32 devices in a mesh: row: 2 (over y), col: 8 (over z, core), orient: 2 (over x).
Axes of the slice: x: 2, y: 2, z: 4, core: 2. Of those that a mesh axis runs over, the one named last changes fastest.
Arguments:
- noise: float32 [2, 4096, 4096], P(None, ('row', 'col')), may hold values from -6 to 6
- elevation_library: float32 [16, 128, 128], replicated, may hold values from 0.25 to 1
- tile_choice_index: int32 [32, 32], P('row', 'col'), may hold values from 0 to 15
- family_heading_index: int32 [8], P('orient'), may hold values from 0 to 35
- family_extent_index: int32 [8], P('orient'), may hold values from 0 to 3
Outputs:
- safety_min: float32 [4096, 4096], P('row', ('col', 'orient'))
The draws below stay inside these ranges and needn't reach their ends.
All inputs are finite; a program needn't handle non-finite values.
Results may differ from the reference program's by a relative error of at most 0.0005.
Values may be sent and summed in bfloat16 or wider, within the bound.
A program may use at most 256 MiB of HBM per device.

```python
import math
import jax
import jax.numpy as jnp
from jax import lax

WINDOW_CELLS = 4096
R = 8
N_AZ = 36
NSIZE = 4
FAM = 8
TILE_SIDE = 128
LIBRARY_TILES = 16
NTILES = 32


def plant(result, stream_key, low, largest):
    longest = result.shape.index(max(result.shape))
    spots = []
    for shift in (0, 1):
        where = [jax.random.randint(jax.random.fold_in(stream_key, axis), (), 0, length) for axis, length in enumerate(result.shape)]
        where[longest] = (where[longest] + shift) % result.shape[longest]
        spots.append(tuple(where))
    return result.at[spots[0]].set(low).at[spots[1]].set(largest)


def block_levels(rng, shape, shards, least, top_value):
    def one(dim, parts):
        steps = jax.random.uniform(jax.random.fold_in(jax.random.fold_in(rng, 6), dim), (parts,), jnp.float32, least / len(shards), top_value / len(shards))
        return jnp.repeat(jnp.exp(steps), shape[dim] // parts).reshape((-1,) + (1,) * (len(shape) - dim - 1))

    factor_of = one(*shards[0])
    for cut in shards[1:]:
        factor_of = factor_of * one(*cut)
    return factor_of


def bell_draw(stream_key, dims, width, most, cuts=(), kind=jnp.bfloat16):
    array = width * jax.random.normal(stream_key, dims, jnp.float32)
    if cuts:
        array = array * block_levels(stream_key, dims, cuts, -0.22, 0.18)
    return jnp.clip(array, -most, most).astype(kind)


def setup_inputs(seed: int = 0) -> dict:
    splits = jax.random.split(jax.random.key(seed), 6)
    noise = bell_draw(splits[0], (2, WINDOW_CELLS, WINDOW_CELLS), 1.0, 6.0, ((1, 16),), jnp.float32)
    elevation_library = jnp.clip(jnp.exp(jax.random.uniform(splits[1], (LIBRARY_TILES, TILE_SIDE, TILE_SIDE), jnp.float32, math.log(0.25), math.log(1.0))), 0.25, 1.0)
    tile_choice_index = plant(jax.random.randint(splits[2], (NTILES, NTILES), 0, LIBRARY_TILES), jax.random.fold_in(splits[2], 1), 0, LIBRARY_TILES - 1).astype(jnp.int32)
    family_heading_index = plant(jax.random.randint(splits[3], (FAM,), 0, N_AZ), jax.random.fold_in(splits[3], 1), 0, N_AZ - 1).astype(jnp.int32)
    family_extent_index = plant(jax.random.randint(splits[4], (FAM,), 0, NSIZE), jax.random.fold_in(splits[4], 1), 0, NSIZE - 1).astype(jnp.int32)
    return dict(noise=noise, elevation_library=elevation_library, tile_choice_index=tile_choice_index, family_heading_index=family_heading_index, family_extent_index=family_extent_index)


nugget_share = 0.3
peak_share = 1024.0 / (2.0 * math.pi)
cutoff_ratio = 32.0

def amplitude(u_index, v_index, side_cells):
    wrap_u = jnp.minimum(u_index, side_cells - u_index).astype(jnp.float32)
    wrap_v = jnp.minimum(v_index, side_cells - v_index).astype(jnp.float32)
    cutoff = side_cells / cutoff_ratio
    scaled_u = wrap_u / cutoff
    scaled_v = wrap_v / cutoff
    grown = 1.0 + scaled_u * scaled_u + scaled_v * scaled_v
    spectrum = nugget_share + peak_share / (grown * jnp.sqrt(grown))
    return jnp.sqrt(spectrum) / side_cells

def ellipsoid(offset_u, offset_v, azimuth, size_index):
    heading = azimuth.astype(jnp.float32) * (math.pi / N_AZ)
    semi_axis = R * (size_index.astype(jnp.float32) + (1 + NSIZE)) / (2 * NSIZE)
    across = 0.6 * semi_axis
    slip_depth = 0.3 * semi_axis
    along = offset_u * jnp.cos(heading) + offset_v * jnp.sin(heading)
    lateral = offset_v * jnp.cos(heading) - offset_u * jnp.sin(heading)
    along_part = along / semi_axis
    lateral_part = lateral / across
    inside = 1.0 - along_part * along_part - lateral_part * lateral_part
    height = slip_depth * jnp.sqrt(jnp.maximum(inside, 0.0))
    base_share = jnp.clip(4.0 * inside, 0.0, 1.0)
    return (height, base_share)

def reference(noise, elevation_library, tile_choice_index, family_heading_index, family_extent_index):
    u_index = lax.broadcasted_iota(jnp.int32, (WINDOW_CELLS, WINDOW_CELLS), 1)
    v_index = lax.broadcasted_iota(jnp.int32, (WINDOW_CELLS, WINDOW_CELLS), 0)
    amplitudes = amplitude(u_index, v_index, WINDOW_CELLS)
    weights = amplitudes * noise[0] + 1j * (amplitudes * noise[1])
    spectral = jnp.fft.fft2(weights)
    field_re = jnp.real(spectral).T
    field_im = jnp.imag(spectral).T
    elevation_tiles = jnp.take(elevation_library, tile_choice_index, axis=0)
    slope_tangents = elevation_tiles.transpose(0, 2, 1, 3).reshape(WINDOW_CELLS, WINDOW_CELLS)
    secant = jnp.sqrt(1.0 + slope_tangents * slope_tangents)
    cohesion = 0.5 * jnp.exp(0.4 * field_re)
    friction = 0.6 * jnp.exp(0.25 * field_im)
    column_terms = jnp.stack([cohesion * secant, friction / secant, slope_tangents / secant])
    column_terms = lax.optimization_barrier(column_terms.astype(jnp.bfloat16)).astype(jnp.float32)
    kernel_width = 2 * R + 1
    offset_u = (lax.broadcasted_iota(jnp.int32, (kernel_width, kernel_width), 0) - R).astype(jnp.float32)
    offset_v = (lax.broadcasted_iota(jnp.int32, (kernel_width, kernel_width), 1) - R).astype(jnp.float32)
    resist_input = column_terms[0:2][None]
    drive_input = column_terms[2:3][None]

    def family_step(family_index, lowest):
        height, base_share = ellipsoid(offset_u, offset_v, family_heading_index[family_index], family_extent_index[family_index])
        height = lax.optimization_barrier(height.astype(jnp.bfloat16)).astype(jnp.float32)
        base_share = lax.optimization_barrier(base_share.astype(jnp.bfloat16)).astype(jnp.float32)
        resist_kernel = jnp.stack([base_share, height])[None]
        drive_kernel = height[None, None]
        resisting = lax.conv_general_dilated(resist_input, resist_kernel, (1, 1), [(R, R), (R, R)], precision=lax.Precision.HIGHEST)[0, 0]
        driving = lax.conv_general_dilated(drive_input, drive_kernel, (1, 1), [(R, R), (R, R)], precision=lax.Precision.HIGHEST)[0, 0]
        return jnp.minimum(lowest, resisting / driving)
    start = jnp.full((WINDOW_CELLS, WINDOW_CELLS), jnp.inf, jnp.float32)
    return lax.fori_loop(0, FAM, family_step, start)
```

```python
import functools
import math

import jax
import jax.numpy as jnp
import numpy as np
from jax import lax
from jax.experimental import pallas as pl
from jax.experimental.pallas import tpu as pltpu
from jax.sharding import PartitionSpec as P

R = 8
N_AZ = 36
NSIZE = 4
LANES = 128
TILE_ROWS = 8
TILE_LANES = 16
GROUPS = LANES // TILE_LANES
PHASE = TILE_ROWS * TILE_LANES

nugget_share = 0.3
peak_share = 1024.0 / (2.0 * math.pi)
cutoff_ratio = 32.0


def amplitude(u_index, v_index, side_cells):
    wrap_u = jnp.minimum(u_index, side_cells - u_index).astype(jnp.float32)
    wrap_v = jnp.minimum(v_index, side_cells - v_index).astype(jnp.float32)
    cutoff = side_cells / cutoff_ratio
    scaled_u = wrap_u / cutoff
    scaled_v = wrap_v / cutoff
    grown = 1.0 + scaled_u * scaled_u + scaled_v * scaled_v
    spectrum = nugget_share + peak_share / (grown * jnp.sqrt(grown))
    return jnp.sqrt(spectrum) / side_cells


def ellipsoid(offset_u, offset_v, azimuth, size_index):
    heading = azimuth.astype(jnp.float32) * (math.pi / N_AZ)
    semi_axis = R * (size_index.astype(jnp.float32) + (1 + NSIZE)) / (2 * NSIZE)
    across = 0.6 * semi_axis
    slip_depth = 0.3 * semi_axis
    along = offset_u * jnp.cos(heading) + offset_v * jnp.sin(heading)
    lateral = offset_v * jnp.cos(heading) - offset_u * jnp.sin(heading)
    along_part = along / semi_axis
    lateral_part = lateral / across
    inside = 1.0 - along_part * along_part - lateral_part * lateral_part
    height = slip_depth * jnp.sqrt(jnp.maximum(inside, 0.0))
    base_share = jnp.clip(4.0 * inside, 0.0, 1.0)
    return (height, base_share)


def small_dft(parts):
    count = len(parts)
    if count == 1:
        return parts
    even = small_dft(parts[0::2])
    odd = small_dft(parts[1::2])
    low, high = [], []
    for k in range(count // 2):
        (a, b), (c, d) = even[k], odd[k]
        if k == 0:
            e, f = c, d
        elif 4 * k == count:
            e, f = d, -c
        else:
            cos = math.cos(2 * math.pi * k / count)
            sin = math.sin(2 * math.pi * k / count)
            e, f = c * cos + d * sin, d * cos - c * sin
        low.append((a + e, b + f))
        high.append((a - e, b - f))
    return low + high


def transform_kernel(planes, blocks, span, step, pad, in_ref, cos_ref, sin_ref, big_ref, small_ref, out_ref, mid, full):
    outer = cos_ref.shape[0]
    rows = mid.shape[1]
    unit = 16 if planes else 8

    @pl.loop(0, rows // unit)
    def _(block):
        at = pl.ds(pl.multiple_of(block * unit, unit), unit)
        parts = []
        for p in range(outer):
            if planes:
                parts.append((in_ref[p, 0, at, :].astype(jnp.float32), in_ref[p, 1, at, :].astype(jnp.float32)))
            else:
                lanes = slice(p * LANES, (p + 1) * LANES)
                parts.append((in_ref[0, at, lanes], in_ref[1, at, lanes]))
        for k, (re, im) in enumerate(small_dft(parts)):
            cos = cos_ref[k : k + 1, :]
            sin = sin_ref[k : k + 1, :]
            mid[k, at, 0:LANES] = re * cos + im * sin
            mid[k, at, LANES : 2 * LANES] = im * cos - re * sin

    if pad:
        edge = jnp.zeros((pad, rows), jnp.float32)
        for part in range(2):
            full[part, 0:pad, :] = edge
            full[part, pad + outer * LANES : 2 * pad + outer * LANES, :] = edge

    turned = (((1,), (1,)), ((), ()))
    dot = functools.partial(lax.dot_general, dimension_numbers=turned, preferred_element_type=jnp.float32)
    for k in range(outer):
        value = mid[k]
        high = value.astype(jnp.bfloat16)
        rest = (value - high.astype(jnp.float32)).astype(jnp.bfloat16)
        got = dot(big_ref[...], high) + dot(big_ref[...], rest) + dot(small_ref[...], high)
        full[0, pl.ds(pad + k, LANES, stride=outer), :] = got[0:LANES]
        full[1, pl.ds(pad + k, LANES, stride=outer), :] = got[LANES : 2 * LANES]

    @pl.loop(0, blocks)
    def _(block):
        at = pl.ds(pl.multiple_of(block * step, 8), span)
        for part in range(2):
            out_ref[block, part] = full[part, at, :].astype(jnp.bfloat16)


def transform(cells, planes, rows, length, blocks, pad):
    outer = length // LANES
    step = length // blocks
    span = step + 2 * pad
    k = np.arange(outer)[:, None]
    q = np.arange(LANES)
    turn = 2 * np.pi * k * q / length
    cos, sin = np.cos(turn).astype(np.float32), np.sin(turn).astype(np.float32)
    angle = 2 * np.pi * (q[:, None] * q % LANES) / LANES
    table = np.block([[np.cos(angle), np.sin(angle)], [-np.sin(angle), np.cos(angle)]]).astype(np.float32)
    big = table.astype(jnp.bfloat16)
    small = (table - big.astype(np.float32)).astype(jnp.bfloat16)
    vmem = pl.BlockSpec(memory_space=pltpu.VMEM)
    return pl.pallas_call(
        functools.partial(transform_kernel, planes, blocks, span, step, pad),
        out_shape=jax.ShapeDtypeStruct((blocks, 2, span, rows), jnp.bfloat16),
        in_specs=[vmem] * 5,
        out_specs=vmem,
        scratch_shapes=[
            pltpu.VMEM((outer, rows, 2 * LANES), jnp.float32),
            pltpu.VMEM((2, length + 2 * pad, rows), jnp.float32),
        ],
        compiler_params=pltpu.CompilerParams(vmem_limit_bytes=40 << 20),
    )(cells, cos, sin, big, small)


def swap_groups(cells):
    row = lax.broadcasted_iota(jnp.int32, cells.shape, 1)
    group = lax.broadcasted_iota(jnp.int32, cells.shape, 2) // TILE_LANES
    for bit in (4, 2, 1):
        row_set = (row & bit) != 0
        group_set = (group & bit) != 0
        lane = bit * TILE_LANES
        down = pltpu.roll(pltpu.roll(cells, TILE_ROWS - bit, 1), lane, 2)
        up = down if bit == 4 else pltpu.roll(pltpu.roll(cells, bit, 1), LANES - lane, 2)
        cells = jnp.where(row_set == group_set, cells, jnp.where(group_set, down, up))
    return cells


def stability_kernel(families, term_ref, band_ref, out_ref, swapped, gathered):
    tiles = gathered.shape[1]
    across = gathered.shape[2]
    chunks = across // GROUPS

    @pl.when(pl.program_id(0) == 0)
    def _():
        @pl.loop(0, tiles // 2)
        def _(pair):
            at = pl.ds(pl.multiple_of(pair * 16, 16), 16)
            for term in range(3):
                for chunk in range(chunks + 1):
                    cells = term_ref[term, at, chunk * LANES : (chunk + 1) * LANES].astype(jnp.float32)
                    turned = swap_groups(cells.reshape(2, TILE_ROWS, LANES))
                    swapped[:, chunk * GROUPS : (chunk + 1) * GROUPS, :] = turned
                both = pl.ds(pair * 2, 2)
                gathered[term, both, :, 0:PHASE] = swapped[:, 0:across, :].astype(jnp.bfloat16)
                gathered[term, both, :, PHASE:] = swapped[:, 1 : across + 1, :].astype(jnp.bfloat16)

    tile = pl.program_id(0) * 2
    low = None
    for pair in range(families // 2):
        lanes = slice(pair * 2 * PHASE, (pair + 1) * 2 * PHASE)
        resisting = driving = None
        for shift in range(3):
            for term in range(3):
                left = gathered[term, pl.ds(tile + shift, 2)].reshape(2 * across, 2 * PHASE)
                got = jnp.dot(left, band_ref[term, shift, :, lanes], preferred_element_type=jnp.float32)
                if term == 2:
                    driving = got if driving is None else driving + got
                else:
                    resisting = got if resisting is None else resisting + got
        ratio = resisting / driving
        least = jnp.minimum(ratio[:, 0:PHASE], ratio[:, PHASE:])
        low = least if low is None else jnp.minimum(low, least)
    turned = swap_groups(low.reshape(2 * chunks, TILE_ROWS, LANES))
    for side in range(2):
        for chunk in range(chunks):
            out_ref[side * 8 : side * 8 + 8, chunk * LANES : (chunk + 1) * LANES] = turned[side * chunks + chunk]


def stability(terms, band, height, width):
    families = band.shape[-1] // PHASE
    across = width // TILE_LANES
    tiles = height // TILE_ROWS + 2
    return pl.pallas_call(
        functools.partial(stability_kernel, families),
        grid=(height // 16,),
        out_shape=jax.ShapeDtypeStruct((height, width), jnp.float32),
        in_specs=[
            pl.BlockSpec(terms.shape, lambda i: (0, 0, 0), pipeline_mode=pl.Buffered(1)),
            pl.BlockSpec(band.shape, lambda i: (0, 0, 0, 0), pipeline_mode=pl.Buffered(1)),
        ],
        out_specs=pl.BlockSpec((16, width), lambda i: (i, 0)),
        scratch_shapes=[
            pltpu.VMEM((2, across + GROUPS, LANES), jnp.float32),
            pltpu.VMEM((3, tiles, across, 2 * PHASE), jnp.bfloat16),
        ],
        compiler_params=pltpu.CompilerParams(vmem_limit_bytes=48 << 20),
    )(terms, band)


def band_weights(headings, extents):
    shape = (3, 2, TILE_ROWS, TILE_LANES, TILE_ROWS, TILE_LANES)
    index = [lax.broadcasted_iota(jnp.int32, shape, axis) for axis in range(6)]
    offset_v = TILE_ROWS * index[0] + index[2] - R - index[4]
    offset_u = TILE_LANES * index[1] + index[3] - R - index[5]
    keep = (jnp.abs(offset_v) <= R) & (jnp.abs(offset_u) <= R)
    rows = 3 * 2 * PHASE

    def flat(cells):
        return cells.reshape(rows, 1, PHASE)

    heights, shares = ellipsoid(
        flat(offset_u.astype(jnp.float32)),
        flat(offset_v.astype(jnp.float32)),
        headings[None, :, None],
        extents[None, :, None],
    )
    keep = flat(keep)
    count = headings.shape[0]

    def whole(cells):
        return jnp.where(keep, cells, 0.0).astype(jnp.bfloat16).reshape(3, 2 * PHASE, count * PHASE)

    heights = whole(heights)
    return jnp.stack([whole(shares), heights, heights])


def body(noise, elevation_library, tile_choice_index, family_heading_index, family_extent_index):
    side_cells = noise.shape[2]
    row_count = lax.axis_size("row")
    col_count = lax.axis_size("col")
    split = lax.axis_size("orient")
    row, col, side = (lax.axis_index(axis) for axis in ("row", "col", "orient"))
    devices = row_count * col_count * split
    lines = noise.shape[1] // split
    window_rows = side_cells // row_count
    window_columns = side_cells // (col_count * split)

    families = lax.all_gather(
        jnp.stack([family_heading_index, family_extent_index]), "orient", axis=1, tiled=True
    )
    choices = lax.all_gather(tile_choice_index, "row", axis=0, tiled=True)
    choices = lax.all_gather(choices, "col", axis=1, tiled=True)

    own = lax.dynamic_slice_in_dim(noise, side * lines, lines, 1)
    first_line = lax.axis_index(("row", "col", "orient")) * lines
    v_index = first_line + lax.broadcasted_iota(jnp.int32, (lines, side_cells), 0)
    u_index = lax.broadcasted_iota(jnp.int32, (lines, side_cells), 1)
    weights = own * amplitude(u_index, v_index, side_cells)[None]
    spectrum = transform(weights, False, lines, side_cells, devices, 0)
    held = lax.all_to_all(spectrum, ("row", "col", "orient"), split_axis=0, concat_axis=0, tiled=True)
    positions = side_cells // devices
    per_block = LANES // lines
    held = held.reshape(side_cells // LANES, per_block, 2, positions, lines)
    held = held.transpose(0, 2, 3, 1, 4).reshape(side_cells // LANES, 2, positions, LANES)
    fields = transform(held, True, positions, side_cells, col_count * split, R)
    fields = lax.all_to_all(fields, ("col", "orient"), split_axis=0, concat_axis=0, tiled=True)
    tall = window_columns + 2 * R
    fields = fields.transpose(1, 2, 0, 3).reshape(2, tall, window_rows)
    ends = row_count - 1
    before = lax.ppermute(fields[:, :, window_rows - R :], "row", [(i, i + 1) for i in range(ends)])
    after = lax.ppermute(fields[:, :, :R], "row", [(i + 1, i) for i in range(ends)])
    wide = (window_rows // LANES + 1) * LANES
    spare = wide - window_rows - 2 * R
    fields = jnp.concatenate(
        [before, fields, after, jnp.zeros((2, tall, spare), fields.dtype)], axis=2
    ).astype(jnp.float32)

    tile_side = elevation_library.shape[1]
    tiles_x = window_rows // tile_side
    tiles_y = window_columns // tile_side
    first_y = col * split + side
    padded_choices = jnp.pad(choices, 1)
    local = lax.dynamic_slice(
        padded_choices, (row * tiles_x, first_y * tiles_y), (tiles_x + 2, tiles_y + 2)
    )
    slope = jnp.take(elevation_library.transpose(0, 2, 1), local.T, axis=0, mode="clip")
    slope = slope.transpose(0, 2, 1, 3).reshape((tiles_y + 2) * tile_side, (tiles_x + 2) * tile_side)
    edge = tile_side - R
    slope = slope[edge : edge + tall, edge : edge + wide]
    y = first_y * window_columns - R + lax.broadcasted_iota(jnp.int32, (tall, wide), 0)
    x = row * window_rows - R + lax.broadcasted_iota(jnp.int32, (tall, wide), 1)
    inside = (y >= 0) & (y < side_cells) & (x >= 0) & (x < side_cells)
    secant = jnp.sqrt(1.0 + slope * slope)
    cohesion = 0.5 * jnp.exp(0.4 * fields[0])
    friction = 0.6 * jnp.exp(0.25 * fields[1])
    terms = jnp.stack([cohesion * secant, friction / secant, slope / secant])
    terms = jnp.where(inside[None], terms, 0.0).astype(jnp.bfloat16)
    band = band_weights(families[0], families[1])
    return stability(terms, band, window_columns, window_rows).T


def solution(mesh):
    placed = (P(None, ("row", "col"), None), P(), P("row", "col"), P("orient"), P("orient"))
    return jax.shard_map(
        body, mesh=mesh, in_specs=placed, out_specs=P("row", ("col", "orient")), check_vma=False
    )
```

```python
import functools
import math

import jax
import jax.numpy as jnp
import numpy as np
from jax import lax
from jax.experimental import pallas as pl
from jax.experimental.pallas import tpu as pltpu
from jax.sharding import PartitionSpec as P

R = 8
N_AZ = 36
NSIZE = 4
LANES = 128
TILE_ROWS = 8
TILE_LANES = 16
GROUPS = LANES // TILE_LANES
PHASE = TILE_ROWS * TILE_LANES
STEP_TILES = 8

nugget_share = 0.3
peak_share = 1024.0 / (2.0 * math.pi)
cutoff_ratio = 32.0


def amplitude(u_index, v_index, side_cells):
    wrap_u = jnp.minimum(u_index, side_cells - u_index).astype(jnp.float32)
    wrap_v = jnp.minimum(v_index, side_cells - v_index).astype(jnp.float32)
    cutoff = side_cells / cutoff_ratio
    scaled_u = wrap_u / cutoff
    scaled_v = wrap_v / cutoff
    grown = 1.0 + scaled_u * scaled_u + scaled_v * scaled_v
    spectrum = nugget_share + peak_share / (grown * jnp.sqrt(grown))
    return jnp.sqrt(spectrum) / side_cells


def ellipsoid(offset_u, offset_v, azimuth, size_index):
    heading = azimuth.astype(jnp.float32) * (math.pi / N_AZ)
    semi_axis = R * (size_index.astype(jnp.float32) + (1 + NSIZE)) / (2 * NSIZE)
    across = 0.6 * semi_axis
    slip_depth = 0.3 * semi_axis
    along = offset_u * jnp.cos(heading) + offset_v * jnp.sin(heading)
    lateral = offset_v * jnp.cos(heading) - offset_u * jnp.sin(heading)
    along_part = along / semi_axis
    lateral_part = lateral / across
    inside = 1.0 - along_part * along_part - lateral_part * lateral_part
    height = slip_depth * jnp.sqrt(jnp.maximum(inside, 0.0))
    base_share = jnp.clip(4.0 * inside, 0.0, 1.0)
    return (height, base_share)


def small_dft(parts):
    count = len(parts)
    if count == 1:
        return parts
    even = small_dft(parts[0::2])
    odd = small_dft(parts[1::2])
    low, high = [], []
    for k in range(count // 2):
        (a, b), (c, d) = even[k], odd[k]
        if k == 0:
            e, f = c, d
        elif 4 * k == count:
            e, f = d, -c
        else:
            cos = math.cos(2 * math.pi * k / count)
            sin = math.sin(2 * math.pi * k / count)
            e, f = c * cos + d * sin, d * cos - c * sin
        low.append((a + e, b + f))
        high.append((a - e, b - f))
    return low + high


def transform_kernel(planes, blocks, span, step, pad, in_ref, cos_ref, sin_ref, big_ref, small_ref, out_ref, mid, full):
    outer = cos_ref.shape[0]
    rows = mid.shape[1]
    unit = 16 if planes else 8

    @pl.loop(0, rows // unit)
    def _(block):
        at = pl.ds(pl.multiple_of(block * unit, unit), unit)
        parts = []
        for p in range(outer):
            if planes:
                parts.append((in_ref[p, 0, at, :].astype(jnp.float32), in_ref[p, 1, at, :].astype(jnp.float32)))
            else:
                lanes = slice(p * LANES, (p + 1) * LANES)
                parts.append((in_ref[0, at, lanes], in_ref[1, at, lanes]))
        for k, (re, im) in enumerate(small_dft(parts)):
            cos = cos_ref[k : k + 1, :]
            sin = sin_ref[k : k + 1, :]
            mid[k, at, 0:LANES] = re * cos + im * sin
            mid[k, at, LANES : 2 * LANES] = im * cos - re * sin

    if pad:
        edge = jnp.zeros((pad, rows), jnp.float32)
        for part in range(2):
            full[part, 0:pad, :] = edge
            full[part, pad + outer * LANES : 2 * pad + outer * LANES, :] = edge

    turned = (((1,), (1,)), ((), ()))
    dot = functools.partial(lax.dot_general, dimension_numbers=turned, preferred_element_type=jnp.float32)
    for k in range(outer):
        value = mid[k]
        high = value.astype(jnp.bfloat16)
        rest = (value - high.astype(jnp.float32)).astype(jnp.bfloat16)
        got = dot(big_ref[...], high) + dot(big_ref[...], rest) + dot(small_ref[...], high)
        full[0, pl.ds(pad + k, LANES, stride=outer), :] = got[0:LANES]
        full[1, pl.ds(pad + k, LANES, stride=outer), :] = got[LANES : 2 * LANES]

    @pl.loop(0, blocks)
    def _(block):
        at = pl.ds(pl.multiple_of(block * step, 8), span)
        for part in range(2):
            out_ref[block, part] = full[part, at, :].astype(jnp.bfloat16)


def transform(cells, planes, rows, length, blocks, pad):
    outer = length // LANES
    step = length // blocks
    span = step + 2 * pad
    k = np.arange(outer)[:, None]
    q = np.arange(LANES)
    turn = 2 * np.pi * k * q / length
    cos, sin = np.cos(turn).astype(np.float32), np.sin(turn).astype(np.float32)
    angle = 2 * np.pi * (q[:, None] * q % LANES) / LANES
    table = np.block([[np.cos(angle), np.sin(angle)], [-np.sin(angle), np.cos(angle)]]).astype(np.float32)
    big = table.astype(jnp.bfloat16)
    small = (table - big.astype(np.float32)).astype(jnp.bfloat16)
    vmem = pl.BlockSpec(memory_space=pltpu.VMEM)
    return pl.pallas_call(
        functools.partial(transform_kernel, planes, blocks, span, step, pad),
        out_shape=jax.ShapeDtypeStruct((blocks, 2, span, rows), jnp.bfloat16),
        in_specs=[vmem] * 5,
        out_specs=vmem,
        scratch_shapes=[
            pltpu.VMEM((outer, rows, 2 * LANES), jnp.float32),
            pltpu.VMEM((2, length + 2 * pad, rows), jnp.float32),
        ],
        compiler_params=pltpu.CompilerParams(vmem_limit_bytes=40 << 20),
    )(cells, cos, sin, big, small)


def swap_groups(cells):
    row = lax.broadcasted_iota(jnp.int32, cells.shape, 1)
    group = lax.broadcasted_iota(jnp.int32, cells.shape, 2) // TILE_LANES
    skewed = pltpu.roll(cells, 0, 2, stride=TILE_LANES, stride_axis=1)
    picked = jnp.take_along_axis(skewed, (group + row - 7) & 7, axis=1)
    level = pltpu.roll(picked, TILE_LANES, 2, stride=TILE_LANES, stride_axis=1)
    return jnp.take_along_axis(level, 7 - row, axis=1)


def stability_kernel(families, term_ref, band_ref, out_ref, swapped, gathered):
    tiles = gathered.shape[1]
    across = gathered.shape[2]
    chunks = across // GROUPS

    @pl.when(pl.program_id(0) == 0)
    def _():
        @pl.loop(0, tiles // 2)
        def _(pair):
            at = pl.ds(pl.multiple_of(pair * 16, 16), 16)
            for term in range(3):
                for chunk in range(chunks + 1):
                    cells = term_ref[term, at, chunk * LANES : (chunk + 1) * LANES].astype(jnp.float32)
                    turned = swap_groups(cells.reshape(2, TILE_ROWS, LANES))
                    swapped[:, chunk * GROUPS : (chunk + 1) * GROUPS, :] = turned
                both = pl.ds(pair * 2, 2)
                gathered[term, both, :, 0:PHASE] = swapped[:, 0:across, :].astype(jnp.bfloat16)
                gathered[term, both, :, PHASE:] = swapped[:, 1 : across + 1, :].astype(jnp.bfloat16)

    tile = pl.program_id(0) * STEP_TILES
    low = None
    for pair in range(families // 2):
        lanes = slice(pair * 2 * PHASE, (pair + 1) * 2 * PHASE)

        def total(chosen):
            pieces = [(term, shift) for term in chosen for shift in range(3)]
            left = [gathered[term, pl.ds(tile + shift, STEP_TILES)] for term, shift in pieces]
            left = [piece.reshape(STEP_TILES * across, 2 * PHASE) for piece in left]
            right = [band_ref[term, shift, :, lanes] for term, shift in pieces]
            return jnp.dot(
                jnp.concatenate(left, axis=1),
                jnp.concatenate(right, axis=0),
                preferred_element_type=jnp.float32,
            )

        ratio = total((0, 1)) / total((2,))
        least = jnp.minimum(ratio[:, 0:PHASE], ratio[:, PHASE:])
        low = least if low is None else jnp.minimum(low, least)
    turned = swap_groups(low.reshape(STEP_TILES * chunks, TILE_ROWS, LANES))
    for side in range(STEP_TILES):
        for chunk in range(chunks):
            out_ref[side * 8 : side * 8 + 8, chunk * LANES : (chunk + 1) * LANES] = turned[side * chunks + chunk]


def stability(terms, band, height, width):
    families = band.shape[-1] // PHASE
    across = width // TILE_LANES
    tiles = height // TILE_ROWS + 2
    return pl.pallas_call(
        functools.partial(stability_kernel, families),
        grid=(height // (TILE_ROWS * STEP_TILES),),
        out_shape=jax.ShapeDtypeStruct((height, width), jnp.float32),
        in_specs=[
            pl.BlockSpec(terms.shape, lambda i: (0, 0, 0), pipeline_mode=pl.Buffered(1)),
            pl.BlockSpec(band.shape, lambda i: (0, 0, 0, 0), pipeline_mode=pl.Buffered(1)),
        ],
        out_specs=pl.BlockSpec((TILE_ROWS * STEP_TILES, width), lambda i: (i, 0)),
        scratch_shapes=[
            pltpu.VMEM((2, across + GROUPS, LANES), jnp.float32),
            pltpu.VMEM((3, tiles, across, 2 * PHASE), jnp.bfloat16),
        ],
        compiler_params=pltpu.CompilerParams(vmem_limit_bytes=56 << 20),
    )(terms, band)


def band_weights(headings, extents):
    shape = (3, 2, TILE_ROWS, TILE_LANES, TILE_ROWS, TILE_LANES)
    index = [lax.broadcasted_iota(jnp.int32, shape, axis) for axis in range(6)]
    offset_v = TILE_ROWS * index[0] + index[2] - R - index[4]
    offset_u = TILE_LANES * index[1] + index[3] - R - index[5]
    keep = (jnp.abs(offset_v) <= R) & (jnp.abs(offset_u) <= R)
    rows = 3 * 2 * PHASE

    def flat(cells):
        return cells.reshape(rows, 1, PHASE)

    heights, shares = ellipsoid(
        flat(offset_u.astype(jnp.float32)),
        flat(offset_v.astype(jnp.float32)),
        headings[None, :, None],
        extents[None, :, None],
    )
    keep = flat(keep)
    count = headings.shape[0]

    def whole(cells):
        return jnp.where(keep, cells, 0.0).astype(jnp.bfloat16).reshape(3, 2 * PHASE, count * PHASE)

    heights = whole(heights)
    return jnp.stack([whole(shares), heights, heights])


def body(noise, elevation_library, tile_choice_index, family_heading_index, family_extent_index):
    side_cells = noise.shape[2]
    row_count = lax.axis_size("row")
    col_count = lax.axis_size("col")
    split = lax.axis_size("orient")
    row, col, side = (lax.axis_index(axis) for axis in ("row", "col", "orient"))
    devices = row_count * col_count * split
    lines = noise.shape[1] // split
    window_rows = side_cells // row_count
    window_columns = side_cells // (col_count * split)

    tiles_down, tiles_over = tile_choice_index.shape
    told = jnp.concatenate(
        [tile_choice_index.reshape(-1), family_heading_index, family_extent_index]
    )
    told = lax.all_gather(told, ("row", "col", "orient"))
    told = told.reshape(row_count, col_count, split, told.shape[1])
    noise, told = lax.optimization_barrier((noise, told))
    area = tiles_down * tiles_over
    choices = told[:, :, 0, :area].reshape(row_count, col_count, tiles_down, tiles_over)
    choices = choices.transpose(0, 2, 1, 3).reshape(row_count * tiles_down, col_count * tiles_over)
    families = told[0, 0, :, area:].reshape(split, 2, -1)
    families = families.transpose(1, 0, 2).reshape(2, -1)

    own = lax.dynamic_slice_in_dim(noise, side * lines, lines, 1)
    first_line = lax.axis_index(("row", "col", "orient")) * lines
    v_index = first_line + lax.broadcasted_iota(jnp.int32, (lines, side_cells), 0)
    u_index = lax.broadcasted_iota(jnp.int32, (lines, side_cells), 1)
    weights = own * amplitude(u_index, v_index, side_cells)[None]
    spectrum = transform(weights, False, lines, side_cells, devices, 0)
    held = lax.all_to_all(spectrum, ("row", "col", "orient"), split_axis=0, concat_axis=0, tiled=True)
    tall = window_columns + 2 * R
    wide = (window_rows // LANES + 1) * LANES
    spare = wide - window_rows - 2 * R
    tile_side = elevation_library.shape[1]
    tiles_x = window_rows // tile_side
    tiles_y = window_columns // tile_side
    first_y = col * split + side
    padded_choices = jnp.pad(choices, 1)
    local = lax.dynamic_slice(
        padded_choices, (row * tiles_x, first_y * tiles_y), (tiles_x + 2, tiles_y + 2)
    )
    slope = jnp.take(elevation_library.transpose(0, 2, 1), local.T, axis=0, mode="clip")
    slope = slope.transpose(0, 2, 1, 3).reshape((tiles_y + 2) * tile_side, (tiles_x + 2) * tile_side)
    edge = tile_side - R
    slope = slope[edge : edge + tall, edge : edge + wide]
    y = first_y * window_columns - R + lax.broadcasted_iota(jnp.int32, (tall, wide), 0)
    x = row * window_rows - R + lax.broadcasted_iota(jnp.int32, (tall, wide), 1)
    inside = (y >= 0) & (y < side_cells) & (x >= 0) & (x < side_cells)
    secant = jnp.sqrt(1.0 + slope * slope)
    lift = jnp.where(inside, 0.5 * secant, 0.0)
    grip = jnp.where(inside, 0.6 / secant, 0.0)
    drive = jnp.where(inside, slope / secant, 0.0).astype(jnp.bfloat16)
    band = band_weights(families[0], families[1])
    held, lift, grip, drive, band = lax.optimization_barrier((held, lift, grip, drive, band))
    positions = side_cells // devices
    per_block = LANES // lines
    held = held.reshape(side_cells // LANES, per_block, 2, positions, lines)
    held = held.transpose(0, 2, 3, 1, 4).reshape(side_cells // LANES, 2, positions, LANES)
    fields = transform(held, True, positions, side_cells, col_count * split, R)
    fields = lax.all_to_all(fields, ("col", "orient"), split_axis=0, concat_axis=0, tiled=True)
    fields = fields.transpose(1, 2, 0, 3).reshape(2, tall, window_rows)
    ends = row_count - 1
    before = lax.ppermute(fields[:, :, window_rows - R :], "row", [(i, i + 1) for i in range(ends)])
    after = lax.ppermute(fields[:, :, :R], "row", [(i + 1, i) for i in range(ends)])
    fields = jnp.concatenate(
        [before, fields, after, jnp.zeros((2, tall, spare), fields.dtype)], axis=2
    ).astype(jnp.float32)

    cohesion = (jnp.exp(0.4 * fields[0]) * lift).astype(jnp.bfloat16)
    friction = (jnp.exp(0.25 * fields[1]) * grip).astype(jnp.bfloat16)
    terms = jnp.stack([cohesion, friction, drive])
    return stability(terms, band, window_columns, window_rows).T


def solution(mesh):
    placed = (P(None, ("row", "col"), None), P(), P("row", "col"), P("orient"), P("orient"))
    return jax.shard_map(
        body, mesh=mesh, in_specs=placed, out_specs=P("row", ("col", "orient")), check_vma=False
    )
```

```python
import functools
import math

import jax
import jax.numpy as jnp
import numpy as np
from jax import lax
from jax.experimental import pallas as pl
from jax.experimental.pallas import tpu as pltpu
from jax.sharding import PartitionSpec as P

R = 8
N_AZ = 36
NSIZE = 4
LANES = 128
TILE_ROWS = 8
TILE_LANES = 16
GROUPS = LANES // TILE_LANES
PHASE = TILE_ROWS * TILE_LANES
STEP_TILES = 8

nugget_share = 0.3
peak_share = 1024.0 / (2.0 * math.pi)
cutoff_ratio = 32.0


def amplitude(u_index, v_index, side_cells):
    wrap_u = jnp.minimum(u_index, side_cells - u_index).astype(jnp.float32)
    wrap_v = jnp.minimum(v_index, side_cells - v_index).astype(jnp.float32)
    cutoff = side_cells / cutoff_ratio
    scaled_u = wrap_u / cutoff
    scaled_v = wrap_v / cutoff
    grown = 1.0 + scaled_u * scaled_u + scaled_v * scaled_v
    spectrum = nugget_share + peak_share / (grown * jnp.sqrt(grown))
    return jnp.sqrt(spectrum) / side_cells


def ellipsoid(offset_u, offset_v, azimuth, size_index):
    heading = azimuth.astype(jnp.float32) * (math.pi / N_AZ)
    semi_axis = R * (size_index.astype(jnp.float32) + (1 + NSIZE)) / (2 * NSIZE)
    across = 0.6 * semi_axis
    slip_depth = 0.3 * semi_axis
    along = offset_u * jnp.cos(heading) + offset_v * jnp.sin(heading)
    lateral = offset_v * jnp.cos(heading) - offset_u * jnp.sin(heading)
    along_part = along / semi_axis
    lateral_part = lateral / across
    inside = 1.0 - along_part * along_part - lateral_part * lateral_part
    height = slip_depth * jnp.sqrt(jnp.maximum(inside, 0.0))
    base_share = jnp.clip(4.0 * inside, 0.0, 1.0)
    return (height, base_share)


def small_dft(parts):
    count = len(parts)
    if count == 1:
        return parts
    even = small_dft(parts[0::2])
    odd = small_dft(parts[1::2])
    low, high = [], []
    for k in range(count // 2):
        (a, b), (c, d) = even[k], odd[k]
        if k == 0:
            e, f = c, d
        elif 4 * k == count:
            e, f = d, -c
        else:
            cos = math.cos(2 * math.pi * k / count)
            sin = math.sin(2 * math.pi * k / count)
            e, f = c * cos + d * sin, d * cos - c * sin
        low.append((a + e, b + f))
        high.append((a - e, b - f))
    return low + high


def transform_kernel(planes, blocks, span, step, pad, in_ref, cos_ref, sin_ref, big_ref, small_ref, out_ref, mid, full):
    outer = cos_ref.shape[0]
    rows = mid.shape[1]
    unit = 16 if planes else 8

    @pl.loop(0, rows // unit)
    def _(block):
        at = pl.ds(pl.multiple_of(block * unit, unit), unit)
        parts = []
        for p in range(outer):
            if planes:
                parts.append((in_ref[p, 0, at, :].astype(jnp.float32), in_ref[p, 1, at, :].astype(jnp.float32)))
            else:
                lanes = slice(p * LANES, (p + 1) * LANES)
                parts.append((in_ref[0, at, lanes], in_ref[1, at, lanes]))
        for k, (re, im) in enumerate(small_dft(parts)):
            cos = cos_ref[k : k + 1, :]
            sin = sin_ref[k : k + 1, :]
            mid[k, at, 0:LANES] = re * cos + im * sin
            mid[k, at, LANES : 2 * LANES] = im * cos - re * sin

    if pad:
        edge = jnp.zeros((pad, rows), jnp.float32)
        for part in range(2):
            full[part, 0:pad, :] = edge
            full[part, pad + outer * LANES : 2 * pad + outer * LANES, :] = edge

    turned = (((1,), (1,)), ((), ()))
    dot = functools.partial(lax.dot_general, dimension_numbers=turned, preferred_element_type=jnp.float32)
    for k in range(outer):
        value = mid[k]
        high = value.astype(jnp.bfloat16)
        rest = (value - high.astype(jnp.float32)).astype(jnp.bfloat16)
        got = dot(big_ref[...], high) + dot(big_ref[...], rest) + dot(small_ref[...], high)
        full[0, pl.ds(pad + k, LANES, stride=outer), :] = got[0:LANES]
        full[1, pl.ds(pad + k, LANES, stride=outer), :] = got[LANES : 2 * LANES]

    @pl.loop(0, blocks)
    def _(block):
        at = pl.ds(pl.multiple_of(block * step, 8), span)
        for part in range(2):
            out_ref[block, part] = full[part, at, :].astype(jnp.bfloat16)


def transform(cells, planes, rows, length, blocks, pad):
    outer = length // LANES
    step = length // blocks
    span = step + 2 * pad
    k = np.arange(outer)[:, None]
    q = np.arange(LANES)
    turn = 2 * np.pi * k * q / length
    cos, sin = np.cos(turn).astype(np.float32), np.sin(turn).astype(np.float32)
    angle = 2 * np.pi * (q[:, None] * q % LANES) / LANES
    table = np.block([[np.cos(angle), np.sin(angle)], [-np.sin(angle), np.cos(angle)]]).astype(np.float32)
    big = table.astype(jnp.bfloat16)
    small = (table - big.astype(np.float32)).astype(jnp.bfloat16)
    vmem = pl.BlockSpec(memory_space=pltpu.VMEM)
    return pl.pallas_call(
        functools.partial(transform_kernel, planes, blocks, span, step, pad),
        out_shape=jax.ShapeDtypeStruct((blocks, 2, span, rows), jnp.bfloat16),
        in_specs=[vmem] * 5,
        out_specs=vmem,
        scratch_shapes=[
            pltpu.VMEM((outer, rows, 2 * LANES), jnp.float32),
            pltpu.VMEM((2, length + 2 * pad, rows), jnp.float32),
        ],
        compiler_params=pltpu.CompilerParams(vmem_limit_bytes=40 << 20),
    )(cells, cos, sin, big, small)


def swap_groups(cells):
    row = lax.broadcasted_iota(jnp.int32, cells.shape, 1)
    group = lax.broadcasted_iota(jnp.int32, cells.shape, 2) // TILE_LANES
    skewed = pltpu.roll(cells, 0, 2, stride=TILE_LANES, stride_axis=1)
    picked = jnp.take_along_axis(skewed, (group + row - 7) & 7, axis=1)
    level = pltpu.roll(picked, TILE_LANES, 2, stride=TILE_LANES, stride_axis=1)
    return jnp.take_along_axis(level, 7 - row, axis=1)


def stability_kernel(families, term_ref, band_ref, out_ref, swapped, gathered):
    tiles = gathered.shape[1]
    across = gathered.shape[2]
    chunks = across // GROUPS

    @pl.when(pl.program_id(0) == 0)
    def _():
        @pl.loop(0, tiles // 2)
        def _(pair):
            at = pl.ds(pl.multiple_of(pair * 16, 16), 16)
            for term in range(3):
                for chunk in range(chunks + 1):
                    cells = term_ref[term, at, chunk * LANES : (chunk + 1) * LANES].astype(jnp.float32)
                    turned = swap_groups(cells.reshape(2, TILE_ROWS, LANES))
                    swapped[:, chunk * GROUPS : (chunk + 1) * GROUPS, :] = turned
                both = pl.ds(pair * 2, 2)
                gathered[term, both, :, 0:PHASE] = swapped[:, 0:across, :].astype(jnp.bfloat16)
                gathered[term, both, :, PHASE:] = swapped[:, 1 : across + 1, :].astype(jnp.bfloat16)

    tile = pl.program_id(0) * STEP_TILES
    low = None
    for pair in range(families // 2):
        lanes = slice(pair * 2 * PHASE, (pair + 1) * 2 * PHASE)

        def total(chosen):
            pieces = [(term, shift) for term in chosen for shift in range(3)]
            left = [gathered[term, pl.ds(tile + shift, STEP_TILES)] for term, shift in pieces]
            left = [piece.reshape(STEP_TILES * across, 2 * PHASE) for piece in left]
            right = [band_ref[term, shift, :, lanes] for term, shift in pieces]
            return jnp.dot(
                jnp.concatenate(left, axis=1),
                jnp.concatenate(right, axis=0),
                preferred_element_type=jnp.float32,
            )

        ratio = total((0, 1)) / total((2,))
        least = jnp.minimum(ratio[:, 0:PHASE], ratio[:, PHASE:])
        low = least if low is None else jnp.minimum(low, least)
    turned = swap_groups(low.reshape(STEP_TILES * chunks, TILE_ROWS, LANES))
    for side in range(STEP_TILES):
        for chunk in range(chunks):
            out_ref[side * 8 : side * 8 + 8, chunk * LANES : (chunk + 1) * LANES] = turned[side * chunks + chunk]


def stability(terms, band, height, width):
    families = band.shape[-1] // PHASE
    across = width // TILE_LANES
    tiles = height // TILE_ROWS + 2
    return pl.pallas_call(
        functools.partial(stability_kernel, families),
        grid=(height // (TILE_ROWS * STEP_TILES),),
        out_shape=jax.ShapeDtypeStruct((height, width), jnp.float32),
        in_specs=[
            pl.BlockSpec(terms.shape, lambda i: (0, 0, 0), pipeline_mode=pl.Buffered(1)),
            pl.BlockSpec(band.shape, lambda i: (0, 0, 0, 0), pipeline_mode=pl.Buffered(1)),
        ],
        out_specs=pl.BlockSpec((TILE_ROWS * STEP_TILES, width), lambda i: (i, 0)),
        scratch_shapes=[
            pltpu.VMEM((2, across + GROUPS, LANES), jnp.float32),
            pltpu.VMEM((3, tiles, across, 2 * PHASE), jnp.bfloat16),
        ],
        compiler_params=pltpu.CompilerParams(vmem_limit_bytes=56 << 20),
    )(terms, band)


def extended(cells, sides, width):
    for axis, dim in sides:
        ends = lax.axis_size(axis) - 1
        head = lax.slice_in_dim(cells, 0, width, axis=dim)
        tail = lax.slice_in_dim(cells, cells.shape[dim] - width, cells.shape[dim], axis=dim)
        before = lax.ppermute(tail, axis, [(i, i + 1) for i in range(ends)])
        after = lax.ppermute(head, axis, [(i + 1, i) for i in range(ends)])
        cells = jnp.concatenate([before, cells, after], axis=dim)
    return cells


def band_weights(headings, extents):
    shape = (3, 2, TILE_ROWS, TILE_LANES, TILE_ROWS, TILE_LANES)
    index = [lax.broadcasted_iota(jnp.int32, shape, axis) for axis in range(6)]
    offset_v = TILE_ROWS * index[0] + index[2] - R - index[4]
    offset_u = TILE_LANES * index[1] + index[3] - R - index[5]
    keep = (jnp.abs(offset_v) <= R) & (jnp.abs(offset_u) <= R)
    rows = 3 * 2 * PHASE

    def flat(cells):
        return cells.reshape(rows, 1, PHASE)

    heights, shares = ellipsoid(
        flat(offset_u.astype(jnp.float32)),
        flat(offset_v.astype(jnp.float32)),
        headings[None, :, None],
        extents[None, :, None],
    )
    keep = flat(keep)
    count = headings.shape[0]

    def whole(cells):
        return jnp.where(keep, cells, 0.0).astype(jnp.bfloat16).reshape(3, 2 * PHASE, count * PHASE)

    heights = whole(heights)
    return jnp.stack([whole(shares), heights, heights])


def body(noise, elevation_library, tile_choice_index, family_heading_index, family_extent_index):
    side_cells = noise.shape[2]
    row_count = lax.axis_size("row")
    col_count = lax.axis_size("col")
    split = lax.axis_size("orient")
    row, col, side = (lax.axis_index(axis) for axis in ("row", "col", "orient"))
    devices = row_count * col_count * split
    lines = noise.shape[1] // split
    window_rows = side_cells // row_count
    window_columns = side_cells // (col_count * split)

    families = jnp.stack([family_heading_index, family_extent_index])
    held_families = [families]
    for turn in range(1, split):
        pairs = [(i, (i + turn) % split) for i in range(split)]
        held_families.append(lax.ppermute(families, "orient", pairs))
    families = jnp.concatenate(held_families, axis=1)
    choices = extended(tile_choice_index, (("row", 0), ("col", 1)), 1)

    own = lax.dynamic_slice_in_dim(noise, side * lines, lines, 1)
    first_line = lax.axis_index(("row", "col", "orient")) * lines
    v_index = first_line + lax.broadcasted_iota(jnp.int32, (lines, side_cells), 0)
    u_index = lax.broadcasted_iota(jnp.int32, (lines, side_cells), 1)
    weights = own * amplitude(u_index, v_index, side_cells)[None]
    spectrum = transform(weights, False, lines, side_cells, devices, 0)
    spectrum, choices, families = lax.optimization_barrier((spectrum, choices, families))
    held = lax.all_to_all(spectrum, ("row", "col", "orient"), split_axis=0, concat_axis=0, tiled=True)
    tall = window_columns + 2 * R
    wide = (window_rows // LANES + 1) * LANES
    spare = wide - window_rows - 2 * R
    tile_side = elevation_library.shape[1]
    tiles_x = window_rows // tile_side
    tiles_y = window_columns // tile_side
    first_y = col * split + side
    local = lax.dynamic_slice_in_dim(choices, side * tiles_y, tiles_y + 2, 1)
    slope = jnp.take(elevation_library.transpose(0, 2, 1), local.T, axis=0, mode="clip")
    slope = slope.transpose(0, 2, 1, 3).reshape((tiles_y + 2) * tile_side, (tiles_x + 2) * tile_side)
    edge = tile_side - R
    slope = slope[edge : edge + tall, edge : edge + wide]
    y = first_y * window_columns - R + lax.broadcasted_iota(jnp.int32, (tall, wide), 0)
    x = row * window_rows - R + lax.broadcasted_iota(jnp.int32, (tall, wide), 1)
    inside = (y >= 0) & (y < side_cells) & (x >= 0) & (x < side_cells)
    secant = jnp.sqrt(1.0 + slope * slope)
    lift = jnp.where(inside, 0.5 * secant, 0.0)
    grip = jnp.where(inside, 0.6 / secant, 0.0)
    drive = jnp.where(inside, slope / secant, 0.0).astype(jnp.bfloat16)
    band = band_weights(families[0], families[1])
    held, lift, grip, drive = lax.optimization_barrier((held, lift, grip, drive))
    positions = side_cells // devices
    per_block = LANES // lines
    held = held.reshape(side_cells // LANES, per_block, 2, positions, lines)
    held = held.transpose(0, 2, 3, 1, 4).reshape(side_cells // LANES, 2, positions, LANES)
    fields = transform(held, True, positions, side_cells, col_count * split, R)
    fields = lax.all_to_all(fields, ("col", "orient"), split_axis=0, concat_axis=0, tiled=True)
    fields = fields.transpose(1, 2, 0, 3).reshape(2, tall, window_rows)
    ends = row_count - 1
    before = lax.ppermute(fields[:, :, window_rows - R :], "row", [(i, i + 1) for i in range(ends)])
    after = lax.ppermute(fields[:, :, :R], "row", [(i + 1, i) for i in range(ends)])
    fields = jnp.concatenate(
        [before, fields, after, jnp.zeros((2, tall, spare), fields.dtype)], axis=2
    ).astype(jnp.float32)

    cohesion = (jnp.exp(0.4 * fields[0]) * lift).astype(jnp.bfloat16)
    friction = (jnp.exp(0.25 * fields[1]) * grip).astype(jnp.bfloat16)
    terms = jnp.stack([cohesion, friction, drive])
    return stability(terms, band, window_columns, window_rows).T


def solution(mesh):
    placed = (P(None, ("row", "col"), None), P(), P("row", "col"), P("orient"), P("orient"))
    return jax.shard_map(
        body, mesh=mesh, in_specs=placed, out_specs=P("row", ("col", "orient")), check_vma=False
    )
```

```python
import functools
import math

import jax
import jax.numpy as jnp
import numpy as np
from jax import lax
from jax.experimental import pallas as pl
from jax.experimental.pallas import tpu as pltpu
from jax.sharding import PartitionSpec as P

R = 8
N_AZ = 36
NSIZE = 4
LANES = 128
TILE_ROWS = 8
TILE_LANES = 16
GROUPS = LANES // TILE_LANES
PHASE = TILE_ROWS * TILE_LANES
STEP_TILES = 8

nugget_share = 0.3
peak_share = 1024.0 / (2.0 * math.pi)
cutoff_ratio = 32.0


def amplitude(u_index, v_index, side_cells):
    wrap_u = jnp.minimum(u_index, side_cells - u_index).astype(jnp.float32)
    wrap_v = jnp.minimum(v_index, side_cells - v_index).astype(jnp.float32)
    cutoff = side_cells / cutoff_ratio
    scaled_u = wrap_u / cutoff
    scaled_v = wrap_v / cutoff
    grown = 1.0 + scaled_u * scaled_u + scaled_v * scaled_v
    spectrum = nugget_share + peak_share / (grown * jnp.sqrt(grown))
    return jnp.sqrt(spectrum) / side_cells


def ellipsoid(offset_u, offset_v, azimuth, size_index):
    heading = azimuth.astype(jnp.float32) * (math.pi / N_AZ)
    semi_axis = R * (size_index.astype(jnp.float32) + (1 + NSIZE)) / (2 * NSIZE)
    across = 0.6 * semi_axis
    slip_depth = 0.3 * semi_axis
    along = offset_u * jnp.cos(heading) + offset_v * jnp.sin(heading)
    lateral = offset_v * jnp.cos(heading) - offset_u * jnp.sin(heading)
    along_part = along / semi_axis
    lateral_part = lateral / across
    inside = 1.0 - along_part * along_part - lateral_part * lateral_part
    height = slip_depth * jnp.sqrt(jnp.maximum(inside, 0.0))
    base_share = jnp.clip(4.0 * inside, 0.0, 1.0)
    return (height, base_share)


def small_dft(parts):
    count = len(parts)
    if count == 1:
        return parts
    even = small_dft(parts[0::2])
    odd = small_dft(parts[1::2])
    low, high = [], []
    for k in range(count // 2):
        (a, b), (c, d) = even[k], odd[k]
        if k == 0:
            e, f = c, d
        elif 4 * k == count:
            e, f = d, -c
        else:
            cos = math.cos(2 * math.pi * k / count)
            sin = math.sin(2 * math.pi * k / count)
            e, f = c * cos + d * sin, d * cos - c * sin
        low.append((a + e, b + f))
        high.append((a - e, b - f))
    return low + high


def transform_kernel(planes, blocks, span, step, pad, in_ref, cos_ref, sin_ref, big_ref, small_ref, out_ref, mid, full):
    outer = cos_ref.shape[0]
    rows = mid.shape[1]
    unit = 16 if planes else 8

    @pl.loop(0, rows // unit)
    def _(block):
        at = pl.ds(pl.multiple_of(block * unit, unit), unit)
        parts = []
        for p in range(outer):
            if planes:
                parts.append((in_ref[p, 0, at, :].astype(jnp.float32), in_ref[p, 1, at, :].astype(jnp.float32)))
            else:
                lanes = slice(p * LANES, (p + 1) * LANES)
                parts.append((in_ref[0, at, lanes], in_ref[1, at, lanes]))
        for k, (re, im) in enumerate(small_dft(parts)):
            cos = cos_ref[k : k + 1, :]
            sin = sin_ref[k : k + 1, :]
            mid[k, at, 0:LANES] = re * cos + im * sin
            mid[k, at, LANES : 2 * LANES] = im * cos - re * sin

    if pad:
        edge = jnp.zeros((pad, rows), jnp.float32)
        for part in range(2):
            full[part, 0:pad, :] = edge
            full[part, pad + outer * LANES : 2 * pad + outer * LANES, :] = edge

    turned = (((1,), (1,)), ((), ()))
    dot = functools.partial(lax.dot_general, dimension_numbers=turned, preferred_element_type=jnp.float32)
    for k in range(outer):
        value = mid[k]
        high = value.astype(jnp.bfloat16)
        rest = (value - high.astype(jnp.float32)).astype(jnp.bfloat16)
        got = dot(big_ref[...], high) + dot(big_ref[...], rest) + dot(small_ref[...], high)
        full[0, pl.ds(pad + k, LANES, stride=outer), :] = got[0:LANES]
        full[1, pl.ds(pad + k, LANES, stride=outer), :] = got[LANES : 2 * LANES]

    @pl.loop(0, blocks)
    def _(block):
        at = pl.ds(pl.multiple_of(block * step, 8), span)
        for part in range(2):
            out_ref[block, part] = full[part, at, :].astype(jnp.bfloat16)


def transform(cells, planes, rows, length, blocks, pad):
    outer = length // LANES
    step = length // blocks
    span = step + 2 * pad
    k = np.arange(outer)[:, None]
    q = np.arange(LANES)
    turn = 2 * np.pi * k * q / length
    cos, sin = np.cos(turn).astype(np.float32), np.sin(turn).astype(np.float32)
    angle = 2 * np.pi * (q[:, None] * q % LANES) / LANES
    table = np.block([[np.cos(angle), np.sin(angle)], [-np.sin(angle), np.cos(angle)]]).astype(np.float32)
    big = table.astype(jnp.bfloat16)
    small = (table - big.astype(np.float32)).astype(jnp.bfloat16)
    vmem = pl.BlockSpec(memory_space=pltpu.VMEM)
    return pl.pallas_call(
        functools.partial(transform_kernel, planes, blocks, span, step, pad),
        out_shape=jax.ShapeDtypeStruct((blocks, 2, span, rows), jnp.bfloat16),
        in_specs=[vmem] * 5,
        out_specs=vmem,
        scratch_shapes=[
            pltpu.VMEM((outer, rows, 2 * LANES), jnp.float32),
            pltpu.VMEM((2, length + 2 * pad, rows), jnp.float32),
        ],
        compiler_params=pltpu.CompilerParams(vmem_limit_bytes=40 << 20),
    )(cells, cos, sin, big, small)


def swap_groups(cells):
    row = lax.broadcasted_iota(jnp.int32, cells.shape, 1)
    group = lax.broadcasted_iota(jnp.int32, cells.shape, 2) // TILE_LANES
    skewed = pltpu.roll(cells, 0, 2, stride=TILE_LANES, stride_axis=1)
    picked = jnp.take_along_axis(skewed, (group + row - 7) & 7, axis=1)
    level = pltpu.roll(picked, TILE_LANES, 2, stride=TILE_LANES, stride_axis=1)
    return jnp.take_along_axis(level, 7 - row, axis=1)


def gather_tiles(term_ref, swapped, gathered):
    tiles, across = gathered.shape[1:3]
    chunks = across // GROUPS

    @pl.when(pl.program_id(0) == 0)
    def _():
        @pl.loop(0, tiles // 2)
        def _(pair):
            at = pl.ds(pl.multiple_of(pair * 16, 16), 16)
            both = pl.ds(pair * 2, 2)
            for term in range(gathered.shape[0]):
                for chunk in range(chunks + 1):
                    cells = term_ref[term, at, chunk * LANES : (chunk + 1) * LANES].astype(jnp.float32)
                    turned = swap_groups(cells.reshape(2, TILE_ROWS, LANES))
                    swapped[:, chunk * GROUPS : (chunk + 1) * GROUPS, :] = turned
                gathered[term, both, :, 0:PHASE] = swapped[:, 0:across, :].astype(jnp.bfloat16)
                gathered[term, both, :, PHASE:] = swapped[:, 1 : across + 1, :].astype(jnp.bfloat16)


def column_sum(gathered, band_ref, lanes):
    terms, _, across, depth = gathered.shape
    tile = pl.program_id(0) * STEP_TILES
    pieces = [(term, shift) for term in range(terms) for shift in range(3)]
    left = [gathered[term, pl.ds(tile + shift, STEP_TILES)] for term, shift in pieces]
    left = [piece.reshape(STEP_TILES * across, depth) for piece in left]
    right = [band_ref[term, shift, :, lanes] for term, shift in pieces]
    return jnp.dot(
        jnp.concatenate(left, axis=1),
        jnp.concatenate(right, axis=0),
        preferred_element_type=jnp.float32,
    )


def driving_kernel(families, term_ref, band_ref, out_ref, swapped, gathered):
    gather_tiles(term_ref, swapped, gathered)
    for pair in range(families // 2):
        lanes = slice(pair * 2 * PHASE, (pair + 1) * 2 * PHASE)
        out_ref[:, lanes] = column_sum(gathered, band_ref, lanes)


def stability_kernel(families, term_ref, band_ref, drive_ref, out_ref, swapped, gathered):
    chunks = gathered.shape[2] // GROUPS
    gather_tiles(term_ref, swapped, gathered)
    low = None
    for pair in range(families // 2):
        lanes = slice(pair * 2 * PHASE, (pair + 1) * 2 * PHASE)
        ratio = column_sum(gathered, band_ref, lanes) / drive_ref[:, lanes]
        least = jnp.minimum(ratio[:, 0:PHASE], ratio[:, PHASE:])
        low = least if low is None else jnp.minimum(low, least)
    turned = swap_groups(low.reshape(STEP_TILES * chunks, TILE_ROWS, LANES))
    for side in range(STEP_TILES):
        for chunk in range(chunks):
            out_ref[side * 8 : side * 8 + 8, chunk * LANES : (chunk + 1) * LANES] = turned[side * chunks + chunk]


def tile_call(kernel, terms, band, height, width, out_shape, out_block, more=()):
    families = band.shape[-1] // PHASE
    across = width // TILE_LANES
    tiles = height // TILE_ROWS + 2
    count = terms.shape[0]
    work = 2 * (height // TILE_ROWS) * across * band.size
    return pl.pallas_call(
        functools.partial(kernel, families),
        grid=(height // (TILE_ROWS * STEP_TILES),),
        out_shape=jax.ShapeDtypeStruct(out_shape, jnp.float32),
        in_specs=[
            pl.BlockSpec(terms.shape, lambda i: (0, 0, 0), pipeline_mode=pl.Buffered(1)),
            pl.BlockSpec(band.shape, lambda i: (0, 0, 0, 0), pipeline_mode=pl.Buffered(1)),
        ]
        + [pl.BlockSpec((STEP_TILES * across, cells.shape[1]), lambda i: (i, 0)) for cells in more],
        out_specs=pl.BlockSpec(out_block, lambda i: (i, 0)),
        scratch_shapes=[
            pltpu.VMEM((2, across + GROUPS, LANES), jnp.float32),
            pltpu.VMEM((count, tiles, across, 2 * PHASE), jnp.bfloat16),
        ],
        compiler_params=pltpu.CompilerParams(vmem_limit_bytes=56 << 20),
        cost_estimate=pl.CostEstimate(flops=work, bytes_accessed=16 << 20, transcendentals=0),
    )(terms, band, *more)


def extended(cells, sides, width):
    for axis, dim in sides:
        ends = lax.axis_size(axis) - 1
        head = lax.slice_in_dim(cells, 0, width, axis=dim)
        tail = lax.slice_in_dim(cells, cells.shape[dim] - width, cells.shape[dim], axis=dim)
        before = lax.ppermute(tail, axis, [(i, i + 1) for i in range(ends)])
        after = lax.ppermute(head, axis, [(i + 1, i) for i in range(ends)])
        cells = jnp.concatenate([before, cells, after], axis=dim)
    return cells


def band_weights(headings, extents):
    shape = (3, 2, TILE_ROWS, TILE_LANES, TILE_ROWS, TILE_LANES)
    index = [lax.broadcasted_iota(jnp.int32, shape, axis) for axis in range(6)]
    offset_v = TILE_ROWS * index[0] + index[2] - R - index[4]
    offset_u = TILE_LANES * index[1] + index[3] - R - index[5]
    keep = (jnp.abs(offset_v) <= R) & (jnp.abs(offset_u) <= R)
    rows = 3 * 2 * PHASE

    def flat(cells):
        return cells.reshape(rows, 1, PHASE)

    heights, shares = ellipsoid(
        flat(offset_u.astype(jnp.float32)),
        flat(offset_v.astype(jnp.float32)),
        headings[None, :, None],
        extents[None, :, None],
    )
    keep = flat(keep)
    count = headings.shape[0]

    def whole(cells):
        return jnp.where(keep, cells, 0.0).astype(jnp.bfloat16).reshape(3, 2 * PHASE, count * PHASE)

    heights = whole(heights)
    return jnp.stack([whole(shares), heights])


def body(noise, elevation_library, tile_choice_index, family_heading_index, family_extent_index):
    side_cells = noise.shape[2]
    row_count = lax.axis_size("row")
    col_count = lax.axis_size("col")
    split = lax.axis_size("orient")
    row, col, side = (lax.axis_index(axis) for axis in ("row", "col", "orient"))
    devices = row_count * col_count * split
    lines = noise.shape[1] // split
    window_rows = side_cells // row_count
    window_columns = side_cells // (col_count * split)

    families = jnp.stack([family_heading_index, family_extent_index])
    held_families = [families]
    for turn in range(1, split):
        pairs = [(i, (i + turn) % split) for i in range(split)]
        held_families.append(lax.ppermute(families, "orient", pairs))
    families = jnp.concatenate(held_families, axis=1)
    choices = extended(tile_choice_index, (("row", 0), ("col", 1)), 1)

    own = lax.dynamic_slice_in_dim(noise, side * lines, lines, 1)
    first_line = lax.axis_index(("row", "col", "orient")) * lines
    v_index = first_line + lax.broadcasted_iota(jnp.int32, (lines, side_cells), 0)
    u_index = lax.broadcasted_iota(jnp.int32, (lines, side_cells), 1)
    weights = own * amplitude(u_index, v_index, side_cells)[None]
    spectrum = transform(weights, False, lines, side_cells, devices, 0)
    spectrum, choices, families = lax.optimization_barrier((spectrum, choices, families))
    held = lax.all_to_all(spectrum, ("row", "col", "orient"), split_axis=0, concat_axis=0, tiled=True)
    tall = window_columns + 2 * R
    wide = (window_rows // LANES + 1) * LANES
    spare = wide - window_rows - 2 * R
    tile_side = elevation_library.shape[1]
    tiles_x = window_rows // tile_side
    tiles_y = window_columns // tile_side
    first_y = col * split + side
    local = lax.dynamic_slice_in_dim(choices, side * tiles_y, tiles_y + 2, 1)
    slope = jnp.take(elevation_library.transpose(0, 2, 1), local.T, axis=0, mode="clip")
    slope = slope.transpose(0, 2, 1, 3).reshape((tiles_y + 2) * tile_side, (tiles_x + 2) * tile_side)
    edge = tile_side - R
    slope = slope[edge : edge + tall, edge : edge + wide]
    y = first_y * window_columns - R + lax.broadcasted_iota(jnp.int32, (tall, wide), 0)
    x = row * window_rows - R + lax.broadcasted_iota(jnp.int32, (tall, wide), 1)
    inside = (y >= 0) & (y < side_cells) & (x >= 0) & (x < side_cells)
    secant = jnp.sqrt(1.0 + slope * slope)
    lift = jnp.where(inside, 0.5 * secant, 0.0)
    grip = jnp.where(inside, 0.6 / secant, 0.0)
    drive = jnp.where(inside, slope / secant, 0.0).astype(jnp.bfloat16)
    band = band_weights(families[0], families[1])
    held, lift, grip, drive = lax.optimization_barrier((held, lift, grip, drive))
    positions = side_cells // devices
    per_block = LANES // lines
    held = held.reshape(side_cells // LANES, per_block, 2, positions, lines)
    held = held.transpose(0, 2, 3, 1, 4).reshape(side_cells // LANES, 2, positions, LANES)
    fields = transform(held, True, positions, side_cells, col_count * split, R)
    fields = lax.all_to_all(fields, ("col", "orient"), split_axis=0, concat_axis=0, tiled=True)
    across = window_rows // TILE_LANES
    driving = tile_call(
        driving_kernel,
        drive[None],
        band[1:],
        window_columns,
        window_rows,
        (window_columns // TILE_ROWS * across, band.shape[-1]),
        (STEP_TILES * across, band.shape[-1]),
    )
    fields, driving, band = lax.optimization_barrier((fields, driving, band))
    fields = fields.transpose(1, 2, 0, 3).reshape(2, tall, window_rows)
    ends = row_count - 1
    before = lax.ppermute(fields[:, :, window_rows - R :], "row", [(i, i + 1) for i in range(ends)])
    after = lax.ppermute(fields[:, :, :R], "row", [(i + 1, i) for i in range(ends)])
    fields = jnp.concatenate(
        [before, fields, after, jnp.zeros((2, tall, spare), fields.dtype)], axis=2
    ).astype(jnp.float32)

    cohesion = (jnp.exp(0.4 * fields[0]) * lift).astype(jnp.bfloat16)
    friction = (jnp.exp(0.25 * fields[1]) * grip).astype(jnp.bfloat16)
    safety = tile_call(
        stability_kernel,
        jnp.stack([cohesion, friction]),
        band,
        window_columns,
        window_rows,
        (window_columns, window_rows),
        (TILE_ROWS * STEP_TILES, window_rows),
        (driving,),
    )
    return safety.T


def solution(mesh):
    placed = (P(None, ("row", "col"), None), P(), P("row", "col"), P("orient"), P("orient"))
    return jax.shard_map(
        body, mesh=mesh, in_specs=placed, out_specs=P("row", ("col", "orient")), check_vma=False
    )
```
